32 devices in a mesh: wide: 16 (over z, y, core), narrow: 2 (over x).
Axes of the slice: x: 2, y: 2, z: 4, core: 2. Of those that a mesh axis runs over, the one named last changes fastest.
Arguments:
- inputs: bfloat16 [18464, 1024], P('wide', 'narrow'), may hold values from -6 to 6
- counts: int32 [16], P('wide'), may hold values from 1 to 2, as said below
- ln1_gain: float32 [1024], P('narrow'), may hold values from 0.5 to 1.5
- ln1_bias: float32 [1024], P('narrow'), may hold values from -3 to 3
- w_qkv: bfloat16 [1024, 3072], P('wide', 'narrow'), may hold values from -2 to 2
- qv_bias: float32 [2048], P('narrow'), may hold values from -3 to 3
- w_proj: bfloat16 [1024, 1024], P('narrow', 'wide'), may hold values from -1.5 to 1.5
- proj_bias: float32 [1024], P('narrow'), may hold values from -3 to 3
- ln2_gain: float32 [1024], P('narrow'), may hold values from 0.5 to 1.5
- ln2_bias: float32 [1024], P('narrow'), may hold values from -3 to 3
- w_fc1: bfloat16 [1024, 4096], P('wide', 'narrow'), may hold values from -0.1875 to 0.1875
- fc1_bias: float32 [4096], P('narrow'), may hold values from -3 to 3
- w_fc2: bfloat16 [4096, 1024], P('narrow', 'wide'), may hold values from -0.09375 to 0.09375
- fc2_bias: float32 [1024], P('narrow'), may hold values from -3 to 3
- cotangent: bfloat16 [18464, 1024], P('wide', 'narrow'), may hold values from -6 to 6
Outputs:
- output: bfloat16 [18464, 1024], P('wide', 'narrow')
- grad_in: bfloat16 [18464, 1024], P('wide', 'narrow')
- grad_ln1_gain: float32 [1024], P('narrow')
- grad_ln1_bias: float32 [1024], P('narrow')
- grad_w_qkv: float32 [1024, 3072], P('wide', 'narrow')
- grad_qv_bias: float32 [2048], P('narrow')
- grad_w_proj: float32 [1024, 1024], P('narrow', 'wide')
- grad_proj_bias: float32 [1024], P('narrow')
- grad_ln2_gain: float32 [1024], P('narrow')
- grad_ln2_bias: float32 [1024], P('narrow')
- grad_w_fc1: float32 [1024, 4096], P('wide', 'narrow')
- grad_fc1_bias: float32 [4096], P('narrow')
- grad_w_fc2: float32 [4096, 1024], P('narrow', 'wide')
- grad_fc2_bias: float32 [1024], P('narrow')
The draws below stay inside these ranges and needn't reach their ends.
Inputs may be any that keep to these rules, and one draw needn't show every extreme that they name: `counts`: each group's images fill its first slots; some group holds 2 images and some holds 1.
All inputs are finite; a program needn't handle non-finite values.
Results may differ from the reference program's by a relative error of at most 0.015.
The reference program's roundings to bfloat16 on the way count: a program that leaves them out, or rounds other values in their place, can miss the bound.
Values may be sent and summed in bfloat16 or wider, within the bound.
A program may use at most 192 MiB of HBM per device.

```python
import math
import jax
import jax.numpy as jnp
from jax import lax

D = 1024
H = 16
DH = 64
FF = 4096
SEQ = 577
IMG_SLOTS = 2
GROUPS = 16
ROWS = 1154
TOKENS = 18464


def draw_counts(key, part):
    drop = jax.random.randint(jax.random.fold_in(key, 1), (GROUPS,), 0, 2)
    counts_drawn = IMG_SLOTS - drop
    first = jax.random.randint(jax.random.fold_in(key, 2), (), 0, GROUPS)
    offset = jax.random.randint(jax.random.fold_in(key, 3), (), 1, GROUPS)
    second = (first + offset) % GROUPS
    counts_drawn = counts_drawn.at[first].set(IMG_SLOTS)
    counts_drawn = counts_drawn.at[second].set(IMG_SLOTS - 1)
    return counts_drawn.astype(jnp.int32)


def draw_w_qkv(key, part):
    base_draw = jax.random.normal(jax.random.fold_in(key, 11), (D, H, 3, DH), jnp.float32)
    base_draw = jnp.clip(base_draw, -6.0, 6.0) / math.sqrt(D)
    return base_draw.reshape(D, 3 * D).astype(jnp.bfloat16)


def block_scale(key, extent, pieces, least, high):
    loudness, own = 1.0, jax.random.fold_in(key, 6)
    for position, shards_of in pieces:
        draws = jnp.exp(jax.random.uniform(jax.random.fold_in(own, position), (shards_of,), jnp.float32, least / len(pieces), high / len(pieces)))
        loudness = loudness * jnp.repeat(draws, extent[position] // shards_of).reshape([-1 if axis == position else 1 for axis in range(len(extent))])
    return loudness


def centred(key, shape, scale, most, shards=(), dtype=jnp.bfloat16):
    drawn = scale * jax.random.normal(key, shape, jnp.float32)
    if shards:
        drawn = drawn * block_scale(key, shape, shards, -0.22, 0.18)
    return jnp.clip(drawn, -most, most).astype(dtype)


def setup_inputs(seed: int = 0) -> dict:
    seeds = jax.random.split(jax.random.key(seed), 16)
    return {
        "inputs": centred(seeds[0], (TOKENS, D), 1.0, 6.0, ((0, 16), (1, 2))),
        "counts": draw_counts(jax.random.fold_in(seeds[15], 71), 0),
        "ln1_gain": jnp.clip(1.0 + 0.1 * jax.random.normal(seeds[2], (D,), jnp.float32), 0.5, 1.5),
        "ln1_bias": centred(seeds[3], (D,), 0.5, 3.0, ((0, 2),), jnp.float32),
        "w_qkv": draw_w_qkv(jax.random.fold_in(seeds[15], 71), 0),
        "qv_bias": centred(seeds[5], (2 * D,), 0.5, 3.0, ((0, 2),), jnp.float32),
        "w_proj": centred(seeds[6], (D, D), (D // 64) ** -0.5, 1.5, ((0, 2), (1, 16))),
        "proj_bias": centred(seeds[7], (D,), 0.5, 3.0, ((0, 2),), jnp.float32),
        "ln2_gain": jnp.clip(1.0 + 0.1 * jax.random.normal(seeds[8], (D,), jnp.float32), 0.5, 1.5),
        "ln2_bias": centred(seeds[9], (D,), 0.5, 3.0, ((0, 2),), jnp.float32),
        "w_fc1": centred(seeds[10], (D, FF), D ** -0.5, 0.1875, ((0, 16), (1, 2))),
        "fc1_bias": centred(seeds[11], (FF,), 0.5, 3.0, ((0, 2),), jnp.float32),
        "w_fc2": centred(seeds[12], (FF, D), FF ** -0.5, 0.09375, ((0, 2), (1, 16))),
        "fc2_bias": centred(seeds[13], (D,), 0.5, 3.0, ((0, 2),), jnp.float32),
        "cotangent": centred(seeds[14], (TOKENS, D), 1.0, 6.0, ((0, 16), (1, 2))),
    }


norm_eps = 1e-06

def normal_cdf(values_in):
    return 0.5 * (1.0 + lax.erf(values_in * (1.0 / math.sqrt(2.0))))

def gelu_exact(values_in):
    return values_in * normal_cdf(values_in)

def gelu_slope(values_in):
    return normal_cdf(values_in) + values_in * jnp.exp(-0.5 * values_in * values_in) * (1.0 / math.sqrt(2.0 * math.pi))

def norm_forward(rows_in, gain_vec, shift_vec):
    center = lax.optimization_barrier(jnp.sum(rows_in, axis=1)) / D
    spread = lax.optimization_barrier(jnp.sum(rows_in * rows_in, axis=1)) / D - center * center
    inv_std = lax.rsqrt(spread + norm_eps)
    normalized = (rows_in - center[:, None]) * inv_std[:, None]
    return (normalized, inv_std, (normalized * gain_vec + shift_vec).astype(jnp.bfloat16))

def norm_backward(incoming, normalized, inv_std, gain_vec):
    scaled = incoming * gain_vec
    first_sum = lax.optimization_barrier(jnp.sum(scaled, axis=1))
    second_sum = lax.optimization_barrier(jnp.sum(scaled * normalized, axis=1))
    back = inv_std[:, None] * (scaled - first_sum[:, None] / D - normalized * (second_sum[:, None] / D))
    return (back, lax.optimization_barrier(jnp.sum(incoming * normalized, axis=0)), lax.optimization_barrier(jnp.sum(incoming, axis=0)))

def ein_float(form, left_mat, right_mat):
    return jnp.einsum(form, left_mat.astype(jnp.float32), right_mat.astype(jnp.float32))

def group_pass(params, group_rows, group_cot, count_live):
    ln1_gain, ln1_bias, w_qkv, qv_bias, w_proj, proj_bias, ln2_gain, ln2_bias, w_fc1, fc1_bias, w_fc2, fc2_bias = params
    slot_count = ROWS // SEQ
    score_scale = 1.0 / math.sqrt(DH)
    slot_of_row = lax.broadcasted_iota(jnp.int32, (ROWS, 1), 0) // SEQ
    live_rows = (slot_of_row < count_live).astype(jnp.float32)
    resid = group_rows.astype(jnp.float32)
    hat_one, inv_one, normed1 = norm_forward(resid, ln1_gain, ln1_bias)
    bias_qv = qv_bias.reshape(H, 2, DH)
    bias_full = jnp.stack([bias_qv[:, 0], jnp.zeros_like(bias_qv[:, 0]), bias_qv[:, 1]], axis=1)
    qkv_rows = jnp.dot(normed1, w_qkv, preferred_element_type=jnp.float32).reshape(ROWS, H, 3, DH) + bias_full
    qkv_rows = qkv_rows.astype(jnp.bfloat16).reshape(slot_count, SEQ, H, 3, DH)
    queries = qkv_rows[:, :, :, 0]
    key_rows = qkv_rows[:, :, :, 1]
    value_rows = qkv_rows[:, :, :, 2]
    scores = ein_float('sqhd,skhd->shqk', queries, key_rows) * score_scale
    row_max = lax.optimization_barrier(jnp.max(scores, axis=-1, keepdims=True))
    exp_scores = jnp.exp(scores - row_max)
    row_total = lax.optimization_barrier(jnp.sum(exp_scores, axis=-1, keepdims=True))
    probs_bf = (exp_scores / row_total).astype(jnp.bfloat16)
    logsum = (row_max + jnp.log(row_total))[..., 0]
    mixed_out = ein_float('shqk,skhd->sqhd', probs_bf, value_rows).astype(jnp.bfloat16)
    mixed_rows = mixed_out.reshape(ROWS, D)
    attn_out = jnp.dot(mixed_rows, w_proj, preferred_element_type=jnp.float32) + proj_bias
    resid_mid = resid + live_rows * attn_out
    hat_two, inv_two, normed2 = norm_forward(resid_mid, ln2_gain, ln2_bias)
    inner_pre = jnp.dot(normed2, w_fc1, preferred_element_type=jnp.float32) + fc1_bias
    activation = gelu_exact(inner_pre).astype(jnp.bfloat16)
    mlp_out = jnp.dot(activation, w_fc2, preferred_element_type=jnp.float32) + fc2_bias
    output = (resid_mid + live_rows * mlp_out).astype(jnp.bfloat16)
    grad_out = group_cot.astype(jnp.float32)
    masked2 = live_rows * grad_out
    sent2 = masked2.astype(jnp.bfloat16)
    grad_w_fc2 = jnp.dot(activation.T, sent2, preferred_element_type=jnp.float32)
    d_inner = jnp.dot(sent2, w_fc2.T, preferred_element_type=jnp.float32) * gelu_slope(inner_pre)
    d_inner_b = d_inner.astype(jnp.bfloat16)
    grad_w_fc1 = jnp.dot(normed2.T, d_inner_b, preferred_element_type=jnp.float32)
    d_norm2 = jnp.dot(d_inner_b, w_fc1.T, preferred_element_type=jnp.float32)
    back_two, grad_ln2_gain, grad_ln2_bias = norm_backward(d_norm2, hat_two, inv_two, ln2_gain)
    d_mid = grad_out + back_two
    masked1 = live_rows * d_mid
    sent1 = masked1.astype(jnp.bfloat16)
    grad_w_proj = jnp.dot(mixed_rows.T, sent1, preferred_element_type=jnp.float32)
    d_mixed = jnp.dot(sent1, w_proj.T, preferred_element_type=jnp.float32).astype(jnp.bfloat16)
    d_mixed = d_mixed.reshape(slot_count, SEQ, H, DH)
    scores_re = ein_float('sqhd,skhd->shqk', queries, key_rows) * score_scale
    probs_re = jnp.exp(scores_re - logsum[..., None])
    d_probs = ein_float('sqhd,skhd->shqk', d_mixed, value_rows)
    row_delta = lax.optimization_barrier(jnp.sum(d_mixed.astype(jnp.float32) * mixed_out.astype(jnp.float32), axis=-1))
    row_delta = jnp.transpose(row_delta, (0, 2, 1))
    d_scores = (probs_re * (d_probs - row_delta[..., None])).astype(jnp.bfloat16)
    d_query = ein_float('shqk,skhd->sqhd', d_scores, key_rows) * score_scale
    d_keys = ein_float('shqk,sqhd->skhd', d_scores, queries) * score_scale
    d_values = ein_float('shqk,sqhd->skhd', probs_re.astype(jnp.bfloat16), d_mixed)
    d_qkv = jnp.stack([d_query, d_keys, d_values], axis=3).reshape(ROWS, 3 * D)
    grad_qv_bias = jnp.stack([lax.optimization_barrier(jnp.sum(d_query, axis=(0, 1))), lax.optimization_barrier(jnp.sum(d_values, axis=(0, 1)))], axis=1).reshape(2 * D)
    d_qkv_b = d_qkv.astype(jnp.bfloat16)
    grad_w_qkv = jnp.dot(normed1.T, d_qkv_b, preferred_element_type=jnp.float32)
    d_norm1 = jnp.dot(d_qkv_b, w_qkv.T, preferred_element_type=jnp.float32)
    back_one, grad_ln1_gain, grad_ln1_bias = norm_backward(d_norm1, hat_one, inv_one, ln1_gain)
    grad_in = (d_mid + back_one).astype(jnp.bfloat16)
    grads = (grad_ln1_gain, grad_ln1_bias, grad_w_qkv, grad_qv_bias, grad_w_proj, lax.optimization_barrier(jnp.sum(masked1, axis=0)), grad_ln2_gain, grad_ln2_bias, grad_w_fc1, lax.optimization_barrier(jnp.sum(d_inner, axis=0)), grad_w_fc2, lax.optimization_barrier(jnp.sum(masked2, axis=0)))
    return ((output, grad_in), grads)

def reference(inputs, counts, ln1_gain, ln1_bias, w_qkv, qv_bias, w_proj, proj_bias, ln2_gain, ln2_bias, w_fc1, fc1_bias, w_fc2, fc2_bias, cotangent):
    params = (ln1_gain, ln1_bias, w_qkv, qv_bias, w_proj, proj_bias, ln2_gain, ln2_bias, w_fc1, fc1_bias, w_fc2, fc2_bias)
    input_groups = inputs.reshape(GROUPS, ROWS, D)
    cot_groups = cotangent.reshape(GROUPS, ROWS, D)

    def group_step(running, scan_item):
        group_rows, group_cot, count_live = scan_item
        outs_pair, grads = group_pass(params, group_rows, group_cot, count_live)
        return (jax.tree.map(lambda first, second: first + second, running, grads), outs_pair)
    zeros_init = tuple((jnp.zeros(param.shape, jnp.float32) for param in params))
    running, (outputs, grads_in) = lax.scan(group_step, zeros_init, (input_groups, cot_groups, counts))
    return (outputs.reshape(TOKENS, D), grads_in.reshape(TOKENS, D), running[0], running[1], running[2], running[3], running[4], running[5], running[6], running[7], running[8], running[9], running[10], running[11])
```

```python
import functools
import math

import jax
import jax.numpy as jnp
from jax import lax
from jax.experimental import pallas as pl
from jax.experimental.pallas import tpu as pltpu
from jax.sharding import PartitionSpec as P

DH = 64
SEQ = 577
ROW_TILE = 16


norm_eps = 1e-06
NT = (((1,), (1,)), ((), ()))
TN = (((0,), (0,)), ((), ()))
NN = (((1,), (0,)), ((), ()))


def dot_f32(left_mat, right_mat, dims=NN):
    return lax.dot_general(left_mat, right_mat, dims, preferred_element_type=jnp.float32)


def swap(piece):
    return lax.ppermute(piece, "narrow", ((0, 1), (1, 0)))


def widen(piece, me, size):
    if size != 2:
        return lax.all_gather(piece, "narrow", axis=1, tiled=True)
    other = swap(piece)
    return jnp.concatenate(
        [jnp.where(me == 0, piece, other), jnp.where(me == 0, other, piece)], axis=1
    )


def sum_whole(partial_rows, size):
    if size != 2:
        return lax.psum(partial_rows, "narrow")
    mine = partial_rows.astype(jnp.bfloat16)
    return mine.astype(jnp.float32) + swap(mine).astype(jnp.float32)


def sum_own(left_mat, right_rows, me, size, width):
    if size != 2:
        return lax.psum_scatter(
            dot_f32(left_mat, right_rows, NT), "narrow", scatter_dimension=1, tiled=True
        )
    theirs = lax.dynamic_slice_in_dim(right_rows, (1 - me) * width, width, 0)
    ours = lax.dynamic_slice_in_dim(right_rows, me * width, width, 0)
    moved = swap(dot_f32(left_mat, theirs, NT).astype(jnp.bfloat16))
    return dot_f32(left_mat, ours, NT) + moved.astype(jnp.float32)


def normal_cdf(values_in):
    return 0.5 * (1.0 + lax.erf(values_in * (1.0 / math.sqrt(2.0))))


def gelu_exact(values_in):
    return values_in * normal_cdf(values_in)


def gelu_slope(values_in):
    return normal_cdf(values_in) + values_in * jnp.exp(-0.5 * values_in * values_in) * (
        1.0 / math.sqrt(2.0 * math.pi)
    )


def norm_forward(rows_in, gain_vec, shift_vec):
    width = float(rows_in.shape[1])
    center = jnp.sum(rows_in, axis=1, keepdims=True) / width
    spread = jnp.sum(rows_in * rows_in, axis=1, keepdims=True) / width - center * center
    inv_std = lax.rsqrt(spread + norm_eps)
    normalized = (rows_in - center) * inv_std
    return (normalized, inv_std, (normalized * gain_vec + shift_vec).astype(jnp.bfloat16))


def scores_by_key(queries, key_rows, score_scale):
    scores = dot_f32(key_rows, queries, NT) * score_scale
    key_index = lax.broadcasted_iota(jnp.int32, scores.shape, 0)
    return jnp.where(key_index < SEQ, scores, -1e30)


def attend_kernel(qkv_ref, mixed_ref, logsum_ref, *, heads, score_scale):
    for head in range(heads):
        base = head * 3 * DH
        queries = qkv_ref[:, base : base + DH]
        key_rows = qkv_ref[:, base + DH : base + 2 * DH]
        value_rows = qkv_ref[:, base + 2 * DH : base + 3 * DH]
        scores = scores_by_key(queries, key_rows, score_scale)
        top = jnp.max(scores, axis=0, keepdims=True)
        exp_scores = jnp.exp(scores - top)
        total = jnp.sum(exp_scores, axis=0, keepdims=True)
        probs = (exp_scores * (1.0 / total)).astype(jnp.bfloat16)
        mixed_ref[:, head * DH : (head + 1) * DH] = dot_f32(probs, value_rows, TN).astype(
            jnp.bfloat16
        )
        logsum_ref[0, head : head + 1, :] = top + jnp.log(total)


def attend_back_kernel(
    qkv_ref, mixed_ref, d_mixed_ref, logsum_ref, d_qkv_ref, sums_ref, *, heads, score_scale
):
    for head in range(heads):
        base = head * 3 * DH
        queries = qkv_ref[:, base : base + DH]
        key_rows = qkv_ref[:, base + DH : base + 2 * DH]
        value_rows = qkv_ref[:, base + 2 * DH : base + 3 * DH]
        mixed = mixed_ref[:, head * DH : (head + 1) * DH]
        d_mixed = d_mixed_ref[:, head * DH : (head + 1) * DH]
        products = d_mixed.astype(jnp.float32) * mixed.astype(jnp.float32)
        delta = jnp.sum(jnp.transpose(products), axis=0, keepdims=True)
        scores = scores_by_key(queries, key_rows, score_scale)
        probs = jnp.exp(scores - logsum_ref[0, head : head + 1, :])
        d_probs = dot_f32(value_rows, d_mixed, NT)
        d_scores = (probs * (d_probs - delta)).astype(jnp.bfloat16)
        d_query = dot_f32(d_scores, key_rows, TN) * score_scale
        d_keys = dot_f32(d_scores, queries, NN) * score_scale
        d_values = dot_f32(probs.astype(jnp.bfloat16), d_mixed, NN)
        for part, grad in enumerate((d_query, d_keys, d_values)):
            columns = slice(base + part * DH, base + (part + 1) * DH)
            d_qkv_ref[:, columns] = grad.astype(jnp.bfloat16)
            sums_ref[0, :, columns] = jnp.broadcast_to(
                jnp.sum(grad, axis=0, keepdims=True), (8, DH)
            )


def head_pairs(width):
    heads = 2
    return heads, width // (3 * DH * heads)


def attend(qkv_rows, slot_rows, score_scale):
    row_count, width = qkv_rows.shape
    slots = row_count // slot_rows
    heads, pairs = head_pairs(width)
    return pl.pallas_call(
        functools.partial(attend_kernel, heads=heads, score_scale=score_scale),
        grid=(slots, pairs),
        in_specs=[pl.BlockSpec((slot_rows, heads * 3 * DH), lambda s, p: (s, p))],
        out_specs=[
            pl.BlockSpec((slot_rows, heads * DH), lambda s, p: (s, p)),
            pl.BlockSpec((1, 8, slot_rows), lambda s, p: (s * pairs + p, 0, 0)),
        ],
        out_shape=[
            jax.ShapeDtypeStruct((row_count, width // 3), jnp.bfloat16),
            jax.ShapeDtypeStruct((slots * pairs, 8, slot_rows), jnp.float32),
        ],
        cost_estimate=pl.CostEstimate(
            flops=4 * slots * pairs * heads * slot_rows * slot_rows * 256,
            bytes_accessed=row_count * width * 3,
            transcendentals=slots * pairs * heads * slot_rows * slot_rows,
        ),
        name="attend",
    )(qkv_rows)


def attend_backward(qkv_rows, mixed_rows, d_mixed, logsum, slot_rows, score_scale):
    row_count, width = qkv_rows.shape
    slots = row_count // slot_rows
    heads, pairs = head_pairs(width)
    narrow_block = pl.BlockSpec((slot_rows, heads * DH), lambda s, p: (s, p))
    wide_block = pl.BlockSpec((slot_rows, heads * 3 * DH), lambda s, p: (s, p))
    return pl.pallas_call(
        functools.partial(attend_back_kernel, heads=heads, score_scale=score_scale),
        grid=(slots, pairs),
        in_specs=[
            wide_block,
            narrow_block,
            narrow_block,
            pl.BlockSpec((1, 8, slot_rows), lambda s, p: (s * pairs + p, 0, 0)),
        ],
        out_specs=[
            wide_block,
            pl.BlockSpec((1, 8, heads * 3 * DH), lambda s, p: (s, 0, p)),
        ],
        out_shape=[
            jax.ShapeDtypeStruct((row_count, width), jnp.bfloat16),
            jax.ShapeDtypeStruct((slots, 8, width), jnp.float32),
        ],
        cost_estimate=pl.CostEstimate(
            flops=10 * slots * pairs * heads * slot_rows * slot_rows * 256,
            bytes_accessed=row_count * width * 6,
            transcendentals=slots * pairs * heads * slot_rows * slot_rows,
        ),
        name="attend_back",
    )(qkv_rows, mixed_rows, d_mixed, logsum)


def shards(
    inputs,
    counts,
    ln1_gain,
    ln1_bias,
    w_qkv,
    qv_bias,
    w_proj,
    proj_bias,
    ln2_gain,
    ln2_bias,
    w_fc1,
    fc1_bias,
    w_fc2,
    fc2_bias,
    cotangent,
):
    size = lax.axis_size("narrow")
    me = lax.axis_index("narrow")
    row_count, width = inputs.shape
    slot_count = row_count // SEQ
    slot_rows = -(-SEQ // ROW_TILE) * ROW_TILE
    padded = slot_count * slot_rows
    head_count = w_qkv.shape[1] // (3 * DH)
    score_scale = 1.0 / math.sqrt(DH)

    def pad_rows(rows):
        rows = rows.reshape(slot_count, SEQ, rows.shape[1])
        rows = jnp.pad(rows, ((0, 0), (0, slot_rows - SEQ), (0, 0)))
        return rows.reshape(padded, rows.shape[2])

    def trim_rows(rows):
        rows = rows.reshape(slot_count, slot_rows, rows.shape[1])[:, :SEQ]
        return rows.reshape(row_count, rows.shape[2])

    def own(rows):
        return lax.dynamic_slice_in_dim(rows, me * width, width, rows.ndim - 1)

    padded_index = lax.broadcasted_iota(jnp.int32, (padded, 1), 0)
    live_rows = (
        (padded_index // slot_rows < counts[0]) & (padded_index % slot_rows < SEQ)
    ).astype(jnp.float32)

    early = lax.all_gather(
        jnp.concatenate([w_qkv, w_proj.T], axis=1), "wide", axis=0, tiled=True
    )
    wqkv_full = early[:, : w_qkv.shape[1]]
    wproj_t = early[:, w_qkv.shape[1] :]
    late = lax.all_gather(
        jnp.concatenate([w_fc1, w_fc2.T], axis=1), "wide", axis=0, tiled=True
    )
    wfc1_full = late[:, : w_fc1.shape[1]]
    wfc2_t = late[:, w_fc1.shape[1] :]

    vectors = widen(
        jnp.stack([ln1_gain, ln1_bias, ln2_gain, ln2_bias, proj_bias]), me, size
    )
    gain_one, shift_one, gain_two, shift_two, proj_shift = (vectors[i : i + 1] for i in range(5))

    inputs_whole = widen(pad_rows(inputs), me, size)
    sent2 = widen((live_rows * pad_rows(cotangent).astype(jnp.float32)).astype(jnp.bfloat16), me, size)

    resid = inputs_whole.astype(jnp.float32)
    hat_one, inv_one, normed1 = norm_forward(resid, gain_one, shift_one)
    bias_qv = qv_bias.reshape(head_count, 2, DH)
    bias_full = jnp.stack(
        [bias_qv[:, 0], jnp.zeros_like(bias_qv[:, 0]), bias_qv[:, 1]], axis=1
    ).reshape(1, head_count * 3 * DH)
    qkv_rows = (dot_f32(normed1, wqkv_full) + bias_full).astype(jnp.bfloat16)
    qkv_rows, sent2 = lax.optimization_barrier((qkv_rows, sent2))
    mixed_rows, logsum = attend(qkv_rows, slot_rows, score_scale)
    attn_out = sum_whole(dot_f32(mixed_rows, wproj_t, NT), size) + proj_shift
    resid_mid = resid + live_rows * attn_out
    hat_two, inv_two, normed2 = norm_forward(resid_mid, gain_two, shift_two)
    inner_pre = dot_f32(normed2, wfc1_full) + fc1_bias
    activation = gelu_exact(inner_pre).astype(jnp.bfloat16)

    d_inner = dot_f32(sent2, wfc2_t) * gelu_slope(inner_pre)
    d_inner_b = d_inner.astype(jnp.bfloat16)
    d_norm2 = sum_whole(dot_f32(d_inner_b, wfc1_full, NT), size)
    grad_fc = jnp.concatenate(
        [
            dot_f32(normed2, d_inner_b, TN).astype(jnp.bfloat16),
            dot_f32(sent2, activation, TN).astype(jnp.bfloat16),
        ],
        axis=1,
    )
    d_norm2, _ = lax.optimization_barrier((d_norm2, grad_fc))
    grad_fc = lax.psum_scatter(grad_fc, "wide", scatter_dimension=0, tiled=True)

    mlp_out = sum_own(activation, wfc2_t, me, size, width) + fc2_bias
    output = trim_rows((own(resid_mid) + live_rows * mlp_out).astype(jnp.bfloat16))

    full_width = float(width * size)
    scaled = d_norm2 * gain_two
    back_two = inv_two * (
        scaled
        - jnp.sum(scaled, axis=1, keepdims=True) / full_width
        - hat_two * (jnp.sum(scaled * hat_two, axis=1, keepdims=True) / full_width)
    )
    own_norm2 = own(d_norm2)
    grad_ln2_gain = jnp.sum(own_norm2 * own(hat_two), axis=0)
    grad_ln2_bias = jnp.sum(own_norm2, axis=0)
    own_cot = pad_rows(cotangent).astype(jnp.float32)
    masked1 = live_rows * (sent2.astype(jnp.float32) + back_two)
    own_mid = own_cot + own(back_two)
    sent1 = masked1.astype(jnp.bfloat16)
    d_mixed = dot_f32(sent1, wproj_t).astype(jnp.bfloat16)
    d_qkv_b, qkv_sums = attend_backward(
        qkv_rows, mixed_rows, d_mixed, logsum, slot_rows, score_scale
    )
    grad_attn = jnp.concatenate(
        [
            dot_f32(normed1, d_qkv_b, TN).astype(jnp.bfloat16),
            dot_f32(sent1, mixed_rows, TN).astype(jnp.bfloat16),
        ],
        axis=1,
    )
    grad_attn = lax.psum_scatter(grad_attn, "wide", scatter_dimension=0, tiled=True)
    qkv_sums = jnp.sum(qkv_sums[:, 0], axis=0).reshape(head_count, 3, DH)
    grad_qv_bias = jnp.stack([qkv_sums[:, 0], qkv_sums[:, 2]], axis=1).reshape(-1)

    part1 = dot_f32(d_qkv_b, wqkv_full, NT)
    scaled_part = part1 * gain_one
    row_sums = jnp.stack([jnp.sum(scaled_part, axis=1), jnp.sum(scaled_part * hat_one, axis=1)])
    if size == 2:
        row_sums = row_sums + swap(row_sums)
        moved = swap(
            lax.dynamic_slice_in_dim(part1, (1 - me) * width, width, 1).astype(jnp.bfloat16)
        )
        d_norm1 = own(part1) + moved.astype(jnp.float32)
    else:
        row_sums = lax.psum(row_sums, "narrow")
        d_norm1 = lax.psum_scatter(part1, "narrow", scatter_dimension=1, tiled=True)
    own_hat = own(hat_one)
    back_one = inv_one * (
        d_norm1 * ln1_gain
        - row_sums[0][:, None] / full_width
        - own_hat * (row_sums[1][:, None] / full_width)
    )
    grad_in = trim_rows((own_mid + back_one).astype(jnp.bfloat16))

    vectors_out = [
        jnp.sum(d_norm1 * own_hat, axis=0),
        jnp.sum(d_norm1, axis=0),
        grad_qv_bias,
        jnp.sum(own(masked1), axis=0),
        grad_ln2_gain,
        grad_ln2_bias,
        jnp.sum(d_inner, axis=0),
        jnp.sum(live_rows * own_cot, axis=0),
    ]
    joined = jnp.concatenate(vectors_out)
    joined = lax.psum(joined.reshape(-1, 128), "wide").reshape(-1)
    summed, at = [], 0
    for vector in vectors_out:
        summed.append(joined[at : at + vector.shape[0]])
        at += vector.shape[0]
    qkv_columns, fc_columns = w_qkv.shape[1], w_fc1.shape[1]
    grad_w_qkv = grad_attn[:, :qkv_columns].astype(jnp.float32)
    grad_w_proj = grad_attn[:, qkv_columns:].T.astype(jnp.float32)
    grad_w_fc1 = grad_fc[:, :fc_columns].astype(jnp.float32)
    grad_w_fc2 = grad_fc[:, fc_columns:].T.astype(jnp.float32)
    return (
        output,
        grad_in,
        summed[0],
        summed[1],
        grad_w_qkv,
        summed[2],
        grad_w_proj,
        summed[3],
        summed[4],
        summed[5],
        grad_w_fc1,
        summed[6],
        grad_w_fc2,
        summed[7],
    )


def solution(mesh):
    return jax.shard_map(
        shards,
        mesh=mesh,
        in_specs=(
            P("wide", "narrow"),
            P("wide"),
            P("narrow"),
            P("narrow"),
            P("wide", "narrow"),
            P("narrow"),
            P("narrow", "wide"),
            P("narrow"),
            P("narrow"),
            P("narrow"),
            P("wide", "narrow"),
            P("narrow"),
            P("narrow", "wide"),
            P("narrow"),
            P("wide", "narrow"),
        ),
        out_specs=(
            P("wide", "narrow"),
            P("wide", "narrow"),
            P("narrow"),
            P("narrow"),
            P("wide", "narrow"),
            P("narrow"),
            P("narrow", "wide"),
            P("narrow"),
            P("narrow"),
            P("narrow"),
            P("wide", "narrow"),
            P("narrow"),
            P("narrow", "wide"),
            P("narrow"),
        ),
        check_vma=False,
    )
```
